256 devices in a mesh: row: 32 (over y, x, core), col: 8 (over z).
Axes of the slice: x: 4, y: 4, z: 8, core: 2. Of those that a mesh axis runs over, the one named last changes fastest.
Arguments:
- hidden: bfloat16 [2048, 2560], P(None, 'row'), may hold values from -6 to 6
- w_qkv: bfloat16 [2560, 3584], P('row', 'col'), may hold values from -8 to 8
- page_table: int32 [64, 64], P('row'), may hold values from -1 to 127, as said below
- prompt_lengths: int32 [64], P('row'), may hold values from 1 to 8192, as said below
- page_keys: bfloat16 [32, 128, 128, 512], P('row', 'col'), may hold values from -4 to 4
- page_values: bfloat16 [32, 128, 128, 512], P('row', 'col'), may hold values from -6 to 6
- tail_lengths: int32 [64, 16], P('row'), may hold values from 0 to 512
- tail_keys: bfloat16 [64, 16, 512, 512], P('row', 'col'), may hold values from -6 to 6
- tail_values: bfloat16 [64, 16, 512, 512], P('row', 'col'), may hold values from -6 to 6
Outputs:
- attended: bfloat16 [64, 16, 2, 2560], P('row', 'col')
The draws below stay inside these ranges and needn't reach their ends.
Inputs may be any that keep to these rules, and one draw needn't show every extreme that they name: `page_table`: entry j of prompt p is the slot of block p // 2 that holds its tokens j * 128 to (j + 1) * 128 - 1 where j * 128 < prompt_lengths[p], else -1; the live slots of a block are distinct. Slot k of a block lies on the device of col index k // 16. The live pages of a block fill the devices' slots one device after another, in an order drawn from the seed, so that at least one device holds 16 live pages. `prompt_lengths`: every block of 2 prompts holds a prompt of 8192 tokens.
All inputs are finite; a program needn't handle non-finite values.
Results may differ from the reference program's by a relative error of at most 0.015.
The reference program's roundings to bfloat16 on the way count: a program that leaves them out, or rounds other values in their place, can miss the bound.
Values may be sent and summed in bfloat16 or wider, within the bound.
A program may use at most 64 MiB of HBM per device.

```python
import math
from functools import partial
import jax
import jax.numpy as jnp
from jax import lax

D = 2560
HEADS = 20
KVH = 4
HD = 128
PAGE = 128
MAXPAGES = 64
SAMPLES = 16
TAIL = 512
PR_DEV = 2
QKV = 3584
KVW = 512
MAXLEN = 8192
PROMPTS = 64
TOKENS = 2048
SLOTS = 128
POOL_DEV = 16


def shuffle_rows(base_key, span_size, number):
    return jax.vmap(partial(jax.random.permutation, x=span_size))(jax.random.split(base_key, number)).astype(jnp.int32)


def layout(key):
    blocks = PROMPTS // PR_DEV
    lengths = jax.random.randint(jax.random.fold_in(key, 101), (blocks, PR_DEV), 1, MAXLEN + 1)
    forced = (POOL_DEV + MAXPAGES - 1) // MAXPAGES
    orders = shuffle_rows(jax.random.fold_in(key, 102), PR_DEV, blocks)
    lengths = jnp.where(orders < forced, MAXLEN, lengths)
    page_counts = (lengths + PAGE - 1) // PAGE
    live_pages = jnp.arange(MAXPAGES)[None, None, :] < page_counts[:, :, None]
    scores = shuffle_rows(jax.random.fold_in(key, 103), SLOTS, blocks).reshape(blocks, PR_DEV, MAXPAGES)
    scores = jnp.where(live_pages, scores, scores + SLOTS).reshape(blocks, SLOTS)
    page_ranks = jnp.argsort(jnp.argsort(scores, axis=1, stable=True), axis=1, stable=True)
    devices = SLOTS // POOL_DEV
    device_order = shuffle_rows(jax.random.fold_in(key, 104), devices, blocks)
    slot_order = shuffle_rows(jax.random.fold_in(key, 105), POOL_DEV, blocks)
    device = jnp.take_along_axis(device_order, page_ranks // POOL_DEV, axis=1)
    within = jnp.take_along_axis(slot_order, page_ranks % POOL_DEV, axis=1)
    entries = jnp.where(live_pages.reshape(blocks, SLOTS), device * POOL_DEV + within, -1)
    return (lengths.reshape(PROMPTS).astype(jnp.int32), entries.reshape(PROMPTS, MAXPAGES).astype(jnp.int32))


def draw_page_table(key, part):
    return layout(key)[1]


def draw_prompt_lengths(key, part):
    return layout(key)[0]


def draw_tail_lengths(key, part):
    flat_counts = jax.random.randint(jax.random.fold_in(key, 201), (PROMPTS * SAMPLES,), 0, TAIL + 1)
    chosen = jax.random.randint(jax.random.fold_in(key, 202), (), 0, PROMPTS * SAMPLES)
    flat_counts = jnp.where(jnp.arange(PROMPTS * SAMPLES) == chosen, TAIL, flat_counts)
    return flat_counts.reshape(PROMPTS, SAMPLES).astype(jnp.int32)


def draw_page_keys(key, part):
    array_shape = (PROMPTS // PR_DEV, SLOTS, PAGE, KVW)
    values = jax.random.truncated_normal(jax.random.fold_in(key, 304), -4.0, 4.0, array_shape, jnp.float32)
    return values.astype(jnp.bfloat16)


def draw_w_qkv(key, part):
    array_shape = (D, QKV)
    values = jax.random.truncated_normal(jax.random.fold_in(key, 403), -4.0, 4.0, array_shape, jnp.float32)
    return (values / jnp.sqrt(jnp.float32(D))).astype(jnp.bfloat16)


def raised(drawn, own_key, source, target, parts, factor):
    def block_of(dim):
        return (jnp.arange(drawn.shape[dim]) // (drawn.shape[dim] // parts)).reshape((-1,) + (1,) * (drawn.ndim - 1 - dim))

    first = jax.random.permutation(own_key, parts)[block_of(target)]
    other_side = (block_of(target) + parts // 2) % parts
    return jnp.where((block_of(source) == first) | (block_of(source) == other_side), factor * drawn, drawn)


def shard_levels(rng, shape, pieces, least, largest):
    def one(position, blocks):
        steps = jax.random.uniform(jax.random.fold_in(jax.random.fold_in(rng, 6), position), (blocks,), jnp.float32, least / len(pieces), largest / len(pieces))
        return jnp.repeat(jnp.exp(steps), shape[position] // blocks).reshape((-1,) + (1,) * (len(shape) - position - 1))

    factor_of = one(*pieces[0])
    for cut in pieces[1:]:
        factor_of = factor_of * one(*cut)
    return factor_of


def noise(stream_key, shape, deviation, bound, cuts=(), held_as=jnp.bfloat16):
    values = deviation * jax.random.normal(stream_key, shape, jnp.float32)
    if cuts:
        values = values * shard_levels(stream_key, shape, cuts, -0.22, 0.18)
    return jnp.clip(values, -bound, bound).astype(held_as)


def heavy_noise(rng, dims, width, most, pieces, heavy, kind=jnp.bfloat16):
    result = width * jax.random.normal(rng, dims, jnp.float32)
    if pieces:
        result = result * shard_levels(rng, dims, pieces, -0.22, 0.18)
    return jnp.clip(raised(result, jax.random.fold_in(rng, 3), *heavy), -most, most).astype(kind)


def setup_inputs(seed: int = 0) -> dict:
    keys = jax.random.split(jax.random.key(seed), 10)
    hidden = heavy_noise(keys[0], (TOKENS, D), 1.0, 6.0, ((1, 32),), (1, 0, 32, 2.75))
    w_qkv = draw_w_qkv(jax.random.fold_in(keys[9], 71), 0)
    page_table = draw_page_table(jax.random.fold_in(keys[9], 71), 0)
    prompt_lengths = draw_prompt_lengths(jax.random.fold_in(keys[9], 71), 0)
    page_keys = draw_page_keys(jax.random.fold_in(keys[9], 71), 0)
    page_values = noise(keys[5], (PROMPTS // PR_DEV, SLOTS, PAGE, KVW), 1.0, 6.0, ((0, 32), (1, 8)))
    tail_lengths = draw_tail_lengths(jax.random.fold_in(keys[9], 71), 0)
    tail_keys = noise(keys[7], (PROMPTS, SAMPLES, TAIL, KVW), 1.0, 6.0, ((0, 32), (1, 8)))
    tail_values = noise(keys[8], (PROMPTS, SAMPLES, TAIL, KVW), 1.0, 6.0, ((0, 32), (1, 8)))
    return dict(hidden=hidden, w_qkv=w_qkv, page_table=page_table, prompt_lengths=prompt_lengths, page_keys=page_keys, page_values=page_values, tail_lengths=tail_lengths, tail_keys=tail_keys, tail_values=tail_values)


rope_base = 500000.0
masked_score = -1e+30

def rounded(values):
    return lax.optimization_barrier(values.astype(jnp.bfloat16))

def rotate(vectors, positions):
    half_size = vectors.shape[-1] // 2
    frequency = jnp.exp(jnp.arange(half_size, dtype=jnp.float32) * (-2.0 * math.log(rope_base) / vectors.shape[-1]))
    angles = positions.astype(jnp.float32)[..., None, None] * frequency
    cosine = jnp.cos(angles)
    sines = jnp.sin(angles)
    leading = vectors[..., :half_size].astype(jnp.float32)
    trailing = vectors[..., half_size:].astype(jnp.float32)
    return jnp.concatenate([leading * cosine - trailing * sines, trailing * cosine + leading * sines], axis=-1)

def reference(hidden, w_qkv, page_table, prompt_lengths, page_keys, page_values, tail_lengths, tail_keys, tail_values):
    group_size = HEADS // KVH
    q_width = HEADS * HD
    kv_width = KVH * HD
    score_scale = 1.0 / math.sqrt(HD)
    projected = rounded(jnp.dot(hidden, w_qkv, preferred_element_type=jnp.float32))
    projected = projected.reshape(PROMPTS, SAMPLES, 2, QKV)
    steps_ahead = jnp.arange(2, dtype=jnp.int32)
    positions = prompt_lengths[:, None, None] + tail_lengths[:, :, None] + steps_ahead[None, None, :]
    queries = rounded(rotate(projected[..., :q_width].reshape(PROMPTS, SAMPLES, 2, HEADS, HD), positions))
    new_keys = rounded(rotate(projected[..., q_width:q_width + kv_width].reshape(PROMPTS, SAMPLES, 2, KVH, HD), positions))
    new_values = projected[..., q_width + kv_width:].reshape(PROMPTS, SAMPLES, 2, KVH, HD)
    causal = steps_ahead[None, :] <= steps_ahead[:, None]

    def one_prompt(inputs):
        prompt, prompt_queries, fresh_keys, fresh_values, tail_counts, tail_rows, tail_vals, table_row, length = inputs
        block_index = (prompt // PR_DEV).astype(jnp.int32)
        pool_keys = lax.dynamic_index_in_dim(page_keys, block_index, 0, keepdims=False)
        pool_values = lax.dynamic_index_in_dim(page_values, block_index, 0, keepdims=False)
        safe_pages = jnp.maximum(table_row, 0)
        key_rows = jnp.take(pool_keys, safe_pages, axis=0).reshape(MAXLEN, KVH, HD).astype(jnp.float32)
        value_rows = jnp.take(pool_values, safe_pages, axis=0).reshape(MAXLEN, KVH, HD).astype(jnp.float32)
        query_grid = prompt_queries.reshape(SAMPLES, 2, KVH, group_size, HD).astype(jnp.float32)
        prefix = jnp.einsum('stkgd,lkd->stkgl', query_grid, key_rows) * score_scale
        prefix = jnp.where(jnp.arange(MAXLEN, dtype=jnp.int32) < length, prefix, masked_score)
        tail_grid = tail_rows.reshape(SAMPLES, TAIL, KVH, HD).astype(jnp.float32)
        tail_scores = jnp.einsum('stkgd,sjkd->stkgj', query_grid, tail_grid) * score_scale
        tail_seen = jnp.arange(TAIL, dtype=jnp.int32)[None, :] < tail_counts[:, None]
        tail_scores = jnp.where(tail_seen[:, None, None, None, :], tail_scores, masked_score)
        fresh_scores = jnp.einsum('stkgd,sukd->stkgu', query_grid, fresh_keys.astype(jnp.float32)) * score_scale
        fresh_scores = jnp.where(causal[None, :, None, None, :], fresh_scores, masked_score)
        scores = jnp.concatenate([prefix, tail_scores, fresh_scores], axis=-1)
        highest = lax.optimization_barrier(jnp.max(scores, axis=-1, keepdims=True))
        weights = jnp.exp(scores - highest)
        totals = lax.optimization_barrier(jnp.sum(weights, axis=-1))
        low_weights = rounded(weights).astype(jnp.float32)
        summed = jnp.einsum('stkgl,lkd->stkgd', low_weights[..., :MAXLEN], value_rows)
        summed = summed + jnp.einsum('stkgj,sjkd->stkgd', low_weights[..., MAXLEN:MAXLEN + TAIL], tail_vals.reshape(SAMPLES, TAIL, KVH, HD).astype(jnp.float32))
        summed = summed + jnp.einsum('stkgu,sukd->stkgd', low_weights[..., MAXLEN + TAIL:], fresh_values.astype(jnp.float32))
        return (summed / totals[..., None]).reshape(SAMPLES, 2, HEADS * HD).astype(jnp.bfloat16)
    inputs = (jnp.arange(PROMPTS, dtype=jnp.int32), queries, new_keys, new_values, tail_lengths, tail_keys, tail_values, page_table, prompt_lengths)
    return lax.map(one_prompt, inputs)
```

```python
import functools
import math

import jax
import jax.numpy as jnp
import numpy as np
from jax import lax
from jax.experimental import pallas as pl
from jax.experimental.pallas import tpu as pltpu
from jax.sharding import PartitionSpec as P

HEADS = 20
KVH = 4
GROUP = HEADS // KVH
HD = 128
NX = 4
NY = 4
NZ = 8
COLS = 448
WA = 256
WB = COLS - WA
KDEV = 80
CHIPS = NX * NY
TOK = 64
SLOTS = 16
PAGE = 128
KEYS = SLOTS * PAGE
TAIL = 512
CHUNK = 512
NCHUNK = KEYS // CHUNK
SCALE = 1.0 / math.sqrt(HD)
ROPE_BASE = 500000.0
LOW = -1e30
MESH = pl.DeviceIdType.MESH
F32 = jnp.float32
BF16 = jnp.bfloat16

W_COPIES = 8 + 2 + 3 * 4 + 4 * 2
H_COPIES = CHIPS - 1
Z_COPIES = 14
M_COPIES = 2 * (NZ - 1)
N_REMOTE = W_COPIES + H_COPIES + 1 + Z_COPIES + M_COPIES


def nt(a, b):
    return lax.dot_general(a, b, (((1,), (1,)), ((), ())), preferred_element_type=F32)


def iota(shape, axis):
    return lax.broadcasted_iota(jnp.int32, shape, axis)


def kernel(
    lengths,
    tails,
    table,
    freq,
    hidden_t,
    weights,
    page_keys,
    page_values,
    tail_keys,
    tail_values,
    out,
    hbuf,
    wa,
    wb,
    xsend,
    xrecv,
    zall,
    kbuf,
    vbuf,
    tkbuf,
    tvbuf,
    cosb,
    sinb,
    bias,
    tbias,
    qrot,
    qown,
    kvown,
    sbuf,
    pack,
    mlpack,
    racc,
    rml,
    send,
    recv,
    local,
):
    row = lax.axis_index("row")
    z = lax.axis_index("col")
    core = lax.rem(row, 2)
    chip = row // 2
    x = lax.rem(chip, NX)
    y = chip // NX
    first = core == 0

    def plane(a, b):
        dx = jnp.where(first, a, b)
        dy = jnp.where(first, b, a)
        there = lax.rem(y + dy, NY) * NX + lax.rem(x + dx, NX)
        return (there * 2 + core, z)

    def along(d):
        return (row, lax.rem(z + d, NZ))

    sibling = (chip * 2 + 1 - core, z)

    locals_ = []

    def fetch(source, target):
        copy = pltpu.make_async_copy(source, target, local.at[len(locals_)])
        copy.start()
        locals_.append(copy)
        return copy

    own_h = fetch(
        hidden_t.at[:, pl.ds(pl.multiple_of(chip * 128, 128), 128)], hbuf.at[pl.ds(0, KDEV)]
    )
    own_wa = fetch(weights.at[:, pl.ds(0, WA)], wa.at[0])
    own_wb = fetch(weights.at[:, pl.ds(WA, WB)], wb.at[0])

    barrier = pltpu.get_barrier_semaphore()
    for a in range(4):
        for b in range(4):
            if (a, b) != (0, 0):
                pl.semaphore_signal(barrier, inc=1, device_id=plane(a, b), device_id_type=MESH)
    pl.semaphore_signal(barrier, inc=1, device_id=sibling, device_id_type=MESH)
    for d in range(1, NZ):
        pl.semaphore_signal(barrier, inc=1, device_id=along(d), device_id_type=MESH)

    page_copies = []
    for k in range(KVH):
        lanes = pl.ds(k * HD, HD)
        page_copies.append(fetch(page_keys.at[0, :, :, lanes], kbuf.at[k]))
        page_copies.append(fetch(page_values.at[0, :, :, lanes], vbuf.at[k]))
    tail_copies = []
    for k in range(KVH):
        lanes = pl.ds(k * HD, HD)
        tail_copies.append(fetch(tail_keys.at[:, :, :, lanes], tkbuf.at[k]))
        tail_copies.append(fetch(tail_values.at[:, :, :, lanes], tvbuf.at[k]))

    pl.semaphore_wait(barrier, CHIPS + NZ - 1)

    remotes = []

    def push(source, target, device):
        at = len(remotes)
        copy = pltpu.make_async_remote_copy(
            src_ref=source,
            dst_ref=target,
            send_sem=send.at[at],
            recv_sem=recv.at[at],
            device_id=device,
            device_id_type=MESH,
        )
        copy.start()
        remotes.append(copy)
        return copy

    def at(a, b):
        return (a % 4) * 4 + (b % 4)

    def w_push(a, b, half, axis, step):
        da, db = (step, 0) if axis == 0 else (0, step)
        buffer = wa if half == 0 else wb
        there = at(a - da, b - db)
        source = buffer.at[at(a, b)]
        if (a, b) == (0, 0):
            source = weights.at[:, pl.ds(0, WA)] if half == 0 else weights.at[:, pl.ds(WA, WB)]
        return push(source, buffer.at[there], plane(da % 4, db % 4))

    got = {}
    for axis in (0, 1):
        for step in (1, -1):
            for half in (0, 1):
                got["own", axis, step, half] = w_push(0, 0, half, axis, step)
    h_copies = []
    for a, b in sorted(
        [(a, b) for a in range(4) for b in range(4) if (a, b) != (0, 0)],
        key=lambda ab: -(min(ab[0], 4 - ab[0]) + min(ab[1], 4 - ab[1])),
    ):
        device = plane(a, b)
        there = device[0] // 2
        h_copies.append(
            push(
                hidden_t.at[:, pl.ds(pl.multiple_of(there * 128, 128), 128)],
                hbuf.at[pl.ds(at(-a, -b) * KDEV, KDEV)],
                device,
            )
        )

    lane = iota((TOK, HD), 1)
    token = iota((TOK, HD), 0)
    position = jnp.zeros((TOK, HD), jnp.int32)
    for c in range(NZ):
        for p in range(2):
            for s in range(2):
                number = c * 4 + p * 2 + s
                value = lengths[p] + tails[p, 2 * c + s]
                position = jnp.where(token // 2 == number, value, position)
    position = position + lax.rem(token, 2)
    angles = position.astype(F32) * freq[...]
    cosb[...] = jnp.cos(angles).reshape(NZ, 8, HD)
    sines = jnp.sin(angles)
    sinb[...] = jnp.where(lane < HD // 2, -sines, sines).reshape(NZ, 8, HD)

    sub = iota((8, PAGE), 0)
    wide = iota((8, PAGE), 1)
    slot_ids = z * SLOTS + iota((SLOTS, 64), 0)
    starts = iota((SLOTS, 64), 1) * PAGE
    seen = []
    for p in range(2):
        hit = table[p : p + 1, :] == slot_ids
        count = jnp.clip(lengths[p] - starts, 0, PAGE)
        seen.append(jnp.sum(jnp.where(hit, count, 0).astype(F32), axis=1, keepdims=True))
    for j in range(SLOTS):
        limit = jnp.where(sub < 4, seen[0][j : j + 1, :], seen[1][j : j + 1, :])
        bias[:, j * PAGE : (j + 1) * PAGE] = jnp.where(wide.astype(F32) < limit, 0.0, LOW)
    tsub = iota((8, TAIL), 0)
    twide = iota((8, TAIL), 1)
    for p in range(2):
        for s in range(2):
            number = p * 2 + s
            count = tails[p, 2 * z + s]
            shown = (tsub // 2 == number) & (twide < count)
            tbias[:, number * TAIL : (number + 1) * TAIL] = jnp.where(shown, 0.0, LOW)

    def arrived(copy):
        copy.wait_recv()

    for step in (1, -1):
        from_a = -step
        for half in (0, 1):
            arrived(got["own", 0, step, half])
        relay_half = 0 if step == 1 else 1
        got["far", relay_half] = w_push(from_a, 0, relay_half, 0, step)
        for half in (0, 1):
            for up in (1, -1):
                got["col", from_a % 4, up, half] = w_push(from_a, 0, half, 1, up)
    for up in (1, -1):
        for half in (0, 1):
            arrived(got["own", 1, up, half])
        relay_half = 0 if up == 1 else 1
        got["relay", 0, relay_half] = w_push(0, -up, relay_half, 1, up)
    for half in (0, 1):
        arrived(got["far", half])
        for up in (1, -1):
            got["col", 2, up, half] = w_push(2, 0, half, 1, up)
    for a in (3, 1, 2):
        for up in (1, -1):
            for half in (0, 1):
                arrived(got["col", a, up, half])
            relay_half = 0 if up == 1 else 1
            got["relay", a, relay_half] = w_push(a, -up, relay_half, 1, up)
    for copy in h_copies:
        arrived(copy)
    own_h.wait()
    own_wa.wait()
    own_wb.wait()
    for a in (0, 3, 1, 2):
        for half in (0, 1):
            arrived(got["relay", a, half])

    new = iota((2 * TOK, 2 * TOK), 0)
    old = iota((2 * TOK, 2 * TOK), 1)
    wanted = (
        (new // 64) * 64
        + lax.rem(new // 4, 2) * 32
        + (lax.rem(new, 64) // 8) * 4
        + lax.rem(new, 4)
    )
    order = jnp.where(wanted == old, 1.0, 0.0).astype(BF16)
    rows = nt(order, hbuf[...]).astype(BF16)
    for half, buffer, width in ((0, wa, WA), (1, wb, WB)):
        part = jnp.dot(
            rows, buffer[...].reshape(CHIPS * KDEV, width), preferred_element_type=F32
        )
        xsend[:, :, half * WA : half * WA + width] = part.reshape(2, TOK, width)
    swap = push(xsend.at[1 - core], xrecv, sibling)
    arrived(swap)
    projected = (xsend[core] + xrecv[...]).astype(BF16)
    zall[z] = projected.reshape(2, TOK // 2, COLS)

    ring = {}

    def z_push(distance, up, part):
        block = lax.rem(z + NZ - up * distance, NZ)
        ring[distance + 1, up, part] = push(
            zall.at[block, part], zall.at[block, part], along(up % NZ)
        )

    for part in (0, 1):
        for up in (1, -1):
            z_push(0, up, part if up == 1 else 1 - part)
    for distance in (1, 2, 3):
        for part in (0, 1):
            for up in (1, -1):
                piece = part if up == 1 else 1 - part
                arrived(ring[distance, up, piece])
                if distance < 3 or part == 0:
                    z_push(distance, up, piece)
    arrived(ring[4, 1, 0])
    arrived(ring[4, -1, 1])

    def head_columns(h):
        begin = h * HD
        block, offset = begin // COLS, begin % COLS
        if offset + HD <= COLS:
            return zall[block, :, :, offset : offset + HD].reshape(TOK, HD)
        cut = COLS - offset
        return jnp.concatenate(
            [
                zall[block, :, :, offset:COLS].reshape(TOK, cut),
                zall[block + 1, :, :, 0 : HD - cut].reshape(TOK, HD - cut),
            ],
            axis=1,
        )

    cosine = cosb[...].reshape(TOK, HD)
    signed = sinb[...].reshape(TOK, HD)

    def turn(values, cosine, signed):
        return values * cosine + pltpu.roll(values, HD // 2, 1) * signed

    for h in range(HEADS):
        k, g = h // GROUP, h % GROUP
        turned = turn(head_columns(h).astype(F32), cosine, signed).astype(BF16)
        qrot[k, g * TOK : (g + 1) * TOK, :] = turned
        qown[h] = turned.astype(F32).reshape(NZ, 8, HD)
    for i in range(2 * KVH):
        kvown[i] = head_columns(HEADS + i).astype(F32).reshape(NZ, 8, HD)

    for copy in page_copies:
        copy.wait()

    lanes = iota((TOK, HD), 1)
    tops = jnp.full((TOK, HD), LOW, F32)
    sums = jnp.zeros((TOK, HD), F32)
    for k in range(KVH):
        query = qrot[k]
        best = jnp.full((GROUP * TOK, PAGE), LOW, F32)
        for i in range(NCHUNK):
            keys = kbuf[k, i * 4 : (i + 1) * 4].reshape(CHUNK, HD)
            scores = nt(query, keys) * SCALE
            scores = (
                scores.reshape(GROUP * NZ, 8, CHUNK)
                + bias[:, i * CHUNK : (i + 1) * CHUNK][None]
            ).reshape(GROUP * TOK, CHUNK)
            sbuf[i] = scores
            for n in range(CHUNK // PAGE):
                best = jnp.maximum(best, scores[:, n * PAGE : (n + 1) * PAGE])
        top = jnp.max(best, axis=1, keepdims=True)
        total = jnp.zeros((GROUP * TOK, PAGE), F32)
        acc = jnp.zeros((GROUP * TOK, HD), F32)
        for i in range(NCHUNK):
            e = jnp.exp(sbuf[i] - top)
            for n in range(CHUNK // PAGE):
                total = total + e[:, n * PAGE : (n + 1) * PAGE]
            acc = acc + jnp.dot(
                e.astype(BF16),
                vbuf[k, i * 4 : (i + 1) * 4].reshape(CHUNK, HD),
                preferred_element_type=F32,
            )
        total = jnp.sum(total, axis=1, keepdims=True)
        for g in range(GROUP):
            h = k * GROUP + g
            part = slice(g * TOK, (g + 1) * TOK)
            pack[:, :, h * HD : (h + 1) * HD] = acc[part].reshape(NZ, 8, HD).astype(BF16)
            tops = jnp.where(lanes == h, top[part], tops)
            sums = jnp.where(lanes == h, total[part], sums)
    mlpack[:, 0] = tops.reshape(NZ, 8, HD)
    mlpack[:, 1] = sums.reshape(NZ, 8, HD)

    states = []
    for d in (4, 3, 5, 2, 6, 1, 7):
        there = lax.rem(z + d, NZ)
        device = along(d)
        states.append(push(pack.at[there], racc.at[NZ - d], device))
        states.append(push(mlpack.at[there], rml.at[NZ - d], device))

    for copy in tail_copies:
        copy.wait()
    fresh_row = iota((8, 16), 0)
    fresh_col = iota((8, 16), 1)
    fresh_shown = (
        (fresh_col < 8)
        & (fresh_row // 2 == fresh_col // 2)
        & (lax.rem(fresh_col, 2) <= lax.rem(fresh_row, 2))
    )
    fresh_bias = jnp.where(fresh_shown, 0.0, LOW)
    nothing = jnp.zeros((8, HD), F32)
    my_cos = cosb[z]
    my_sin = sinb[z]
    small = iota((8, HD), 1)
    own_tops = jnp.full((8, HD), LOW, F32)
    own_sums = jnp.zeros((8, HD), F32)
    own_acc = []
    for k in range(KVH):
        query = jnp.concatenate([qown[k * GROUP + g, z] for g in range(GROUP)], axis=0)
        query = query.astype(BF16)
        new_key = turn(kvown[k, z], my_cos, my_sin)
        new_key = jnp.concatenate([new_key, nothing], axis=0).astype(BF16)
        new_value = jnp.concatenate([kvown[KVH + k, z], nothing], axis=0).astype(BF16)
        scores = nt(query, tkbuf[k].reshape(KEYS, HD)) * SCALE
        scores = scores.reshape(GROUP, 8, KEYS) + tbias[...][None]
        scores = scores.reshape(GROUP * 8, KEYS)
        fresh = nt(query, new_key) * SCALE
        fresh = (fresh.reshape(GROUP, 8, 16) + fresh_bias[None]).reshape(GROUP * 8, 16)
        top = jnp.maximum(
            jnp.max(scores, axis=1, keepdims=True), jnp.max(fresh, axis=1, keepdims=True)
        )
        e = jnp.exp(scores - top)
        f = jnp.exp(fresh - top)
        total = jnp.sum(e, axis=1, keepdims=True) + jnp.sum(f, axis=1, keepdims=True)
        acc = jnp.dot(
            e.astype(BF16), tvbuf[k].reshape(KEYS, HD), preferred_element_type=F32
        ) + jnp.dot(f.astype(BF16), new_value, preferred_element_type=F32)
        for g in range(GROUP):
            h = k * GROUP + g
            part = slice(g * 8, (g + 1) * 8)
            own_acc.append(acc[part])
            own_tops = jnp.where(small == h, top[part], own_tops)
            own_sums = jnp.where(small == h, total[part], own_sums)

    for copy in states:
        arrived(copy)
    racc[0] = pack[z]
    rml[0] = mlpack[z]
    best = own_tops
    for i in range(NZ):
        best = jnp.maximum(best, rml[i, 0])
    factors = [jnp.exp(own_tops - best)]
    total = factors[0] * own_sums
    for i in range(NZ):
        factor = jnp.exp(rml[i, 0] - best)
        factors.append(factor)
        total = total + factor * rml[i, 1]
    for h in range(HEADS):
        column = slice(h * HD, (h + 1) * HD)
        acc = factors[0][:, h : h + 1] * own_acc[h]
        for i in range(NZ):
            acc = acc + factors[i + 1][:, h : h + 1] * racc[i, :, column].astype(F32)
        out[:, column] = (acc / total[:, h : h + 1]).astype(BF16)

    for copy in remotes:
        copy.wait_send()


def local_step(
    hidden,
    w_qkv,
    page_table,
    prompt_lengths,
    page_keys,
    page_values,
    tail_lengths,
    tail_keys,
    tail_values,
):
    half = np.arange(HD // 2, dtype=np.float64)
    one = np.exp(half * (-2.0 * math.log(ROPE_BASE) / HD)).astype(np.float32)
    freq = jnp.asarray(np.concatenate([one, one])[None])
    smem = pl.BlockSpec(memory_space=pltpu.SMEM)
    vmem = pl.BlockSpec(memory_space=pltpu.VMEM)
    hbm = pl.BlockSpec(memory_space=pl.ANY)
    attended = pl.pallas_call(
        kernel,
        out_shape=jax.ShapeDtypeStruct((8, HEADS * HD), BF16),
        in_specs=[smem, smem, vmem, vmem] + [hbm] * 6,
        out_specs=vmem,
        scratch_shapes=[
            pltpu.VMEM((CHIPS * KDEV, 2 * TOK), BF16),
            pltpu.VMEM((CHIPS, KDEV, WA), BF16),
            pltpu.VMEM((CHIPS, KDEV, WB), BF16),
            pltpu.VMEM((2, TOK, COLS), F32),
            pltpu.VMEM((TOK, COLS), F32),
            pltpu.VMEM((NZ, 2, TOK // 2, COLS), BF16),
            pltpu.VMEM((KVH, SLOTS, PAGE, HD), BF16),
            pltpu.VMEM((KVH, SLOTS, PAGE, HD), BF16),
            pltpu.VMEM((KVH, 2, 2, TAIL, HD), BF16),
            pltpu.VMEM((KVH, 2, 2, TAIL, HD), BF16),
            pltpu.VMEM((NZ, 8, HD), F32),
            pltpu.VMEM((NZ, 8, HD), F32),
            pltpu.VMEM((8, KEYS), F32),
            pltpu.VMEM((8, KEYS), F32),
            pltpu.VMEM((KVH, GROUP * TOK, HD), BF16),
            pltpu.VMEM((HEADS, NZ, 8, HD), F32),
            pltpu.VMEM((2 * KVH, NZ, 8, HD), F32),
            pltpu.VMEM((NCHUNK, GROUP * TOK, CHUNK), F32),
            pltpu.VMEM((NZ, 8, HEADS * HD), BF16),
            pltpu.VMEM((NZ, 2, 8, HD), F32),
            pltpu.VMEM((NZ, 8, HEADS * HD), BF16),
            pltpu.VMEM((NZ, 2, 8, HD), F32),
            pltpu.SemaphoreType.DMA((N_REMOTE,)),
            pltpu.SemaphoreType.DMA((N_REMOTE,)),
            pltpu.SemaphoreType.DMA((3 + 4 * KVH,)),
        ],
        compiler_params=pltpu.CompilerParams(
            collective_id=0, has_side_effects=True, vmem_limit_bytes=56 << 20
        ),
        name="decode",
    )(
        prompt_lengths,
        tail_lengths,
        page_table,
        freq,
        hidden.T,
        w_qkv,
        page_keys,
        page_values,
        tail_keys,
        tail_values,
    )
    return attended.reshape(2, 2, 2, HEADS * HD)


def solution(mesh):
    in_specs = (
        P(None, "row"),
        P("row", "col"),
        P("row", None),
        P("row"),
        P("row", "col", None, None),
        P("row", "col", None, None),
        P("row", None),
        P("row", "col", None, None),
        P("row", "col", None, None),
    )
    out_specs = P("row", "col", None, None)
    return jax.shard_map(
        local_step, mesh=mesh, in_specs=in_specs, out_specs=out_specs, check_vma=False
    )
```

```python
import functools
import math

import jax
import jax.numpy as jnp
import numpy as np
from jax import lax
from jax.experimental import pallas as pl
from jax.experimental.pallas import tpu as pltpu
from jax.sharding import PartitionSpec as P

HEADS = 20
KVH = 4
GROUP = HEADS // KVH
HD = 128
NX = 4
NY = 4
NZ = 8
COLS = 448
WA = 256
WB = COLS - WA
KDEV = 80
CHIPS = NX * NY
TOK = 64
SLOTS = 16
PAGE = 128
KEYS = SLOTS * PAGE
TAIL = 512
CHUNK = 512
NCHUNK = KEYS // CHUNK
SCALE = 1.0 / math.sqrt(HD)
ROPE_BASE = 500000.0
LOW = -1e30
MESH = pl.DeviceIdType.MESH
F32 = jnp.float32
BF16 = jnp.bfloat16

W_COPIES = 8 + 2 + 3 * 4 + 4 * 2
H_COPIES = CHIPS - 1
PARTS = 2
ROWS = TOK // PARTS
Z_COPIES = 7 * PARTS
KCOLS = GROUP * HD
M_COPIES = (KVH // 2 + 1) * (NZ - 1)
N_REMOTE = W_COPIES + H_COPIES + 1 + Z_COPIES + M_COPIES


def nt(a, b):
    return lax.dot_general(a, b, (((1,), (1,)), ((), ())), preferred_element_type=F32)


def iota(shape, axis):
    return lax.broadcasted_iota(jnp.int32, shape, axis)


def kernel(
    lengths,
    tails,
    table,
    freq,
    hidden_t,
    weights,
    page_keys,
    page_values,
    tail_keys,
    tail_values,
    out,
    hbuf,
    wa,
    wb,
    xsend,
    xrecv,
    zall,
    kbuf,
    vbuf,
    tkbuf,
    tvbuf,
    cosb,
    sinb,
    bias,
    tbias,
    qrot,
    qown,
    kvown,
    sbuf,
    pack,
    mlpack,
    racc,
    rml,
    send,
    recv,
    local,
):
    row = lax.axis_index("row")
    z = lax.axis_index("col")
    core = lax.rem(row, 2)
    chip = row // 2
    x = lax.rem(chip, NX)
    y = chip // NX
    first = core == 0

    def plane(a, b):
        dx = jnp.where(first, a, b)
        dy = jnp.where(first, b, a)
        there = lax.rem(y + dy, NY) * NX + lax.rem(x + dx, NX)
        return (there * 2 + core, z)

    def along(d):
        return (row, lax.rem(z + d, NZ))

    sibling = (chip * 2 + 1 - core, z)

    locals_ = []

    def fetch(source, target):
        copy = pltpu.make_async_copy(source, target, local.at[len(locals_)])
        copy.start()
        locals_.append(copy)
        return copy

    own_h = fetch(
        hidden_t.at[:, pl.ds(pl.multiple_of(chip * 128, 128), 128)], hbuf.at[pl.ds(0, KDEV)]
    )
    own_wa = fetch(weights.at[:, pl.ds(0, WA)], wa.at[0])
    own_wb = fetch(weights.at[:, pl.ds(WA, WB)], wb.at[0])

    barrier = pltpu.get_barrier_semaphore()
    for a in range(4):
        for b in range(4):
            if (a, b) != (0, 0):
                pl.semaphore_signal(barrier, inc=1, device_id=plane(a, b), device_id_type=MESH)
    pl.semaphore_signal(barrier, inc=1, device_id=sibling, device_id_type=MESH)
    for d in range(1, NZ):
        pl.semaphore_signal(barrier, inc=1, device_id=along(d), device_id_type=MESH)

    page_copies = []
    for k in range(KVH):
        lanes = pl.ds(k * HD, HD)
        page_copies.append(fetch(page_keys.at[0, :, :, lanes], kbuf.at[k]))
        page_copies.append(fetch(page_values.at[0, :, :, lanes], vbuf.at[k]))
    tail_copies = []
    for k in range(KVH):
        lanes = pl.ds(k * HD, HD)
        tail_copies.append(fetch(tail_keys.at[:, :, :, lanes], tkbuf.at[k]))
        tail_copies.append(fetch(tail_values.at[:, :, :, lanes], tvbuf.at[k]))

    pl.semaphore_wait(barrier, CHIPS + NZ - 1)

    remotes = []

    def push(source, target, device):
        at = len(remotes)
        copy = pltpu.make_async_remote_copy(
            src_ref=source,
            dst_ref=target,
            send_sem=send.at[at],
            recv_sem=recv.at[at],
            device_id=device,
            device_id_type=MESH,
        )
        copy.start()
        remotes.append(copy)
        return copy

    def at(a, b):
        return (a % 4) * 4 + (b % 4)

    def w_push(a, b, half, axis, step):
        da, db = (step, 0) if axis == 0 else (0, step)
        buffer = wa if half == 0 else wb
        there = at(a - da, b - db)
        source = buffer.at[at(a, b)]
        if (a, b) == (0, 0):
            source = weights.at[:, pl.ds(0, WA)] if half == 0 else weights.at[:, pl.ds(WA, WB)]
        return push(source, buffer.at[there], plane(da % 4, db % 4))

    got = {}
    for axis in (0, 1):
        for step in (1, -1):
            for half in (0, 1):
                got["own", axis, step, half] = w_push(0, 0, half, axis, step)
    h_copies = []
    for a, b in sorted(
        [(a, b) for a in range(4) for b in range(4) if (a, b) != (0, 0)],
        key=lambda ab: -(min(ab[0], 4 - ab[0]) + min(ab[1], 4 - ab[1])),
    ):
        device = plane(a, b)
        there = device[0] // 2
        h_copies.append(
            push(
                hidden_t.at[:, pl.ds(pl.multiple_of(there * 128, 128), 128)],
                hbuf.at[pl.ds(at(-a, -b) * KDEV, KDEV)],
                device,
            )
        )

    lane = iota((TOK, HD), 1)
    token = iota((TOK, HD), 0)
    position = jnp.zeros((TOK, HD), jnp.int32)
    for c in range(NZ):
        for p in range(2):
            for s in range(2):
                number = c * 4 + p * 2 + s
                value = lengths[p] + tails[p, 2 * c + s]
                position = jnp.where(token // 2 == number, value, position)
    position = position + lax.rem(token, 2)
    angles = position.astype(F32) * freq[...]
    cosb[...] = jnp.cos(angles).reshape(NZ, 8, HD)
    sines = jnp.sin(angles)
    sinb[...] = jnp.where(lane < HD // 2, -sines, sines).reshape(NZ, 8, HD)

    sub = iota((8, PAGE), 0)
    wide = iota((8, PAGE), 1)
    slot_ids = z * SLOTS + iota((SLOTS, 64), 0)
    starts = iota((SLOTS, 64), 1) * PAGE
    seen = []
    for p in range(2):
        hit = table[p : p + 1, :] == slot_ids
        count = jnp.clip(lengths[p] - starts, 0, PAGE)
        seen.append(jnp.sum(jnp.where(hit, count, 0).astype(F32), axis=1, keepdims=True))
    for j in range(SLOTS):
        limit = jnp.where(sub < 4, seen[0][j : j + 1, :], seen[1][j : j + 1, :])
        bias[:, j * PAGE : (j + 1) * PAGE] = jnp.where(wide.astype(F32) < limit, 0.0, LOW)
    tsub = iota((8, TAIL), 0)
    twide = iota((8, TAIL), 1)
    for p in range(2):
        for s in range(2):
            number = p * 2 + s
            count = tails[p, 2 * z + s]
            shown = (tsub // 2 == number) & (twide < count)
            tbias[:, number * TAIL : (number + 1) * TAIL] = jnp.where(shown, 0.0, LOW)

    def arrived(copy):
        copy.wait_recv()

    for step in (1, -1):
        from_a = -step
        for half in (0, 1):
            arrived(got["own", 0, step, half])
        relay_half = 0 if step == 1 else 1
        got["far", relay_half] = w_push(from_a, 0, relay_half, 0, step)
        for half in (0, 1):
            for up in (1, -1):
                got["col", from_a % 4, up, half] = w_push(from_a, 0, half, 1, up)
    for up in (1, -1):
        for half in (0, 1):
            arrived(got["own", 1, up, half])
        relay_half = 0 if up == 1 else 1
        got["relay", 0, relay_half] = w_push(0, -up, relay_half, 1, up)
    for half in (0, 1):
        arrived(got["far", half])
        for up in (1, -1):
            got["col", 2, up, half] = w_push(2, 0, half, 1, up)
    for a in (3, 1, 2):
        for up in (1, -1):
            for half in (0, 1):
                arrived(got["col", a, up, half])
            relay_half = 0 if up == 1 else 1
            got["relay", a, relay_half] = w_push(a, -up, relay_half, 1, up)
    for copy in h_copies:
        arrived(copy)
    own_h.wait()
    own_wa.wait()
    own_wb.wait()
    for a in (0, 3, 1, 2):
        for half in (0, 1):
            arrived(got["relay", a, half])

    new = iota((2 * TOK, 2 * TOK), 0)
    old = iota((2 * TOK, 2 * TOK), 1)
    wanted = (
        (new // 64) * 64
        + lax.rem(new // 4, 2) * 32
        + (lax.rem(new, 64) // 8) * 4
        + lax.rem(new, 4)
    )
    order = jnp.where(wanted == old, 1.0, 0.0).astype(BF16)
    rows = nt(order, hbuf[...]).astype(BF16)
    for half, buffer, width in ((0, wa, WA), (1, wb, WB)):
        part = jnp.dot(
            rows, buffer[...].reshape(CHIPS * KDEV, width), preferred_element_type=F32
        )
        xsend[:, :, half * WA : half * WA + width] = part.reshape(2, TOK, width)
    swap = push(xsend.at[1 - core], xrecv, sibling)
    arrived(swap)
    projected = (xsend[core] + xrecv[...]).astype(BF16)
    zall[z] = projected.reshape(PARTS, ROWS, COLS)

    ring = {}

    def z_push(distance, up, part):
        block = lax.rem(z + NZ - up * distance, NZ)
        ring[distance + 1, up, part] = push(
            zall.at[block, part], zall.at[block, part], along(up % NZ)
        )

    def piece_of(part, up):
        return part if up == 1 else (part + PARTS // 2) % PARTS

    for part in range(PARTS):
        for up in (1, -1):
            z_push(0, up, piece_of(part, up))
    for distance in (1, 2, 3):
        for part in range(PARTS):
            for up in (1, -1):
                piece = piece_of(part, up)
                arrived(ring[distance, up, piece])
                if distance < 3 or part < PARTS // 2:
                    z_push(distance, up, piece)
    for part in range(PARTS // 2):
        for up in (1, -1):
            arrived(ring[4, up, piece_of(part, up)])

    def head_columns(h):
        begin = h * HD
        block, offset = begin // COLS, begin % COLS
        if offset + HD <= COLS:
            return zall[block, :, :, offset : offset + HD].reshape(TOK, HD)
        cut = COLS - offset
        return jnp.concatenate(
            [
                zall[block, :, :, offset:COLS].reshape(TOK, cut),
                zall[block + 1, :, :, 0 : HD - cut].reshape(TOK, HD - cut),
            ],
            axis=1,
        )

    cosine = cosb[...].reshape(TOK, HD)
    signed = sinb[...].reshape(TOK, HD)

    def turn(values, cosine, signed):
        return values * cosine + pltpu.roll(values, HD // 2, 1) * signed

    for h in range(HEADS):
        k, g = h // GROUP, h % GROUP
        turned = turn(head_columns(h).astype(F32), cosine, signed).astype(BF16)
        qrot[k, g * TOK : (g + 1) * TOK, :] = turned
        qown[h] = turned.astype(F32).reshape(NZ, 8, HD)
    for i in range(2 * KVH):
        kvown[i] = head_columns(HEADS + i).astype(F32).reshape(NZ, 8, HD)

    for copy in page_copies:
        copy.wait()

    states = []
    lanes = iota((TOK, HD), 1)
    mlpack[...] = jnp.full((NZ, 8, HD), LOW, F32)

    def attend(k):
        both = mlpack[...].reshape(TOK, HD)
        query = qrot[k]
        best = jnp.full((GROUP * TOK, PAGE), LOW, F32)
        for i in range(NCHUNK):
            keys = kbuf[k, i * 4 : (i + 1) * 4].reshape(CHUNK, HD)
            scores = nt(query, keys) * SCALE
            scores = (
                scores.reshape(GROUP * NZ, 8, CHUNK)
                + bias[:, i * CHUNK : (i + 1) * CHUNK][None]
            ).reshape(GROUP * TOK, CHUNK)
            sbuf[i] = scores
            for n in range(CHUNK // PAGE):
                best = jnp.maximum(best, scores[:, n * PAGE : (n + 1) * PAGE])
        top = jnp.max(best, axis=1, keepdims=True)
        total = jnp.zeros((GROUP * TOK, PAGE), F32)
        acc = jnp.zeros((GROUP * TOK, HD), F32)
        for i in range(NCHUNK):
            e = jnp.exp(sbuf[i] - top)
            for n in range(CHUNK // PAGE):
                total = total + e[:, n * PAGE : (n + 1) * PAGE]
            acc = acc + jnp.dot(
                e.astype(BF16),
                vbuf[k, i * 4 : (i + 1) * 4].reshape(CHUNK, HD),
                preferred_element_type=F32,
            )
        total = jnp.sum(total, axis=1, keepdims=True)
        for g in range(GROUP):
            h = k * GROUP + g
            part = slice(g * TOK, (g + 1) * TOK)
            pack[:, :, h * HD : (h + 1) * HD] = acc[part].reshape(NZ, 8, HD).astype(BF16)
            both = jnp.where(lanes == h, top[part], both)
            both = jnp.where(lanes == h + HD // 2, total[part], both)
        mlpack[...] = both.reshape(NZ, 8, HD)

    for k in range(KVH):
        pl.when(z >= 0)(functools.partial(attend, k))
        if k % 2 == 0:
            continue
        columns = pl.ds((k - 1) * KCOLS, 2 * KCOLS)
        for d in (4, 3, 5, 2, 6, 1, 7):
            there = lax.rem(z + d, NZ)
            source = pack.at[there, :, columns]
            states.append(push(source, racc.at[NZ - d, :, columns], along(d)))
    for d in (4, 3, 5, 2, 6, 1, 7):
        there = lax.rem(z + d, NZ)
        states.append(push(mlpack.at[there], rml.at[NZ - d], along(d)))
    for copy in tail_copies:
        copy.wait()
    fresh_row = iota((8, 16), 0)
    fresh_col = iota((8, 16), 1)
    fresh_shown = (
        (fresh_col < 8)
        & (fresh_row // 2 == fresh_col // 2)
        & (lax.rem(fresh_col, 2) <= lax.rem(fresh_row, 2))
    )
    fresh_bias = jnp.where(fresh_shown, 0.0, LOW)
    nothing = jnp.zeros((8, HD), F32)
    my_cos = cosb[z]
    my_sin = sinb[z]
    small = iota((8, HD), 1)
    own_tops = jnp.full((8, HD), LOW, F32)
    own_sums = jnp.zeros((8, HD), F32)
    own_acc = []
    for k in range(KVH):
        query = jnp.concatenate([qown[k * GROUP + g, z] for g in range(GROUP)], axis=0)
        query = query.astype(BF16)
        new_key = turn(kvown[k, z], my_cos, my_sin)
        new_key = jnp.concatenate([new_key, nothing], axis=0).astype(BF16)
        new_value = jnp.concatenate([kvown[KVH + k, z], nothing], axis=0).astype(BF16)
        scores = nt(query, tkbuf[k].reshape(KEYS, HD)) * SCALE
        scores = scores.reshape(GROUP, 8, KEYS) + tbias[...][None]
        scores = scores.reshape(GROUP * 8, KEYS)
        fresh = nt(query, new_key) * SCALE
        fresh = (fresh.reshape(GROUP, 8, 16) + fresh_bias[None]).reshape(GROUP * 8, 16)
        top = jnp.maximum(
            jnp.max(scores, axis=1, keepdims=True), jnp.max(fresh, axis=1, keepdims=True)
        )
        e = jnp.exp(scores - top)
        f = jnp.exp(fresh - top)
        total = jnp.sum(e, axis=1, keepdims=True) + jnp.sum(f, axis=1, keepdims=True)
        acc = jnp.dot(
            e.astype(BF16), tvbuf[k].reshape(KEYS, HD), preferred_element_type=F32
        ) + jnp.dot(f.astype(BF16), new_value, preferred_element_type=F32)
        for g in range(GROUP):
            h = k * GROUP + g
            part = slice(g * 8, (g + 1) * 8)
            own_acc.append(acc[part])
            own_tops = jnp.where(small == h, top[part], own_tops)
            own_sums = jnp.where(small == h, total[part], own_sums)

    for copy in states:
        arrived(copy)
    racc[0] = pack[z]
    rml[0] = mlpack[z]
    best = own_tops
    for i in range(NZ):
        best = jnp.maximum(best, rml[i])
    factors = [jnp.exp(own_tops - best)]
    total = factors[0] * own_sums
    for i in range(NZ):
        factor = jnp.exp(rml[i] - best)
        factors.append(factor)
        total = total + factor * pltpu.roll(rml[i], HD // 2, 1)
    for h in range(HEADS):
        column = slice(h * HD, (h + 1) * HD)
        acc = factors[0][:, h : h + 1] * own_acc[h]
        for i in range(NZ):
            acc = acc + factors[i + 1][:, h : h + 1] * racc[i, :, column].astype(F32)
        out[:, column] = (acc / total[:, h : h + 1]).astype(BF16)

    for copy in remotes:
        copy.wait_send()


def local_step(
    hidden,
    w_qkv,
    page_table,
    prompt_lengths,
    page_keys,
    page_values,
    tail_lengths,
    tail_keys,
    tail_values,
):
    half = np.arange(HD // 2, dtype=np.float64)
    one = np.exp(half * (-2.0 * math.log(ROPE_BASE) / HD)).astype(np.float32)
    freq = jnp.asarray(np.concatenate([one, one])[None])
    smem = pl.BlockSpec(memory_space=pltpu.SMEM)
    vmem = pl.BlockSpec(memory_space=pltpu.VMEM)
    hbm = pl.BlockSpec(memory_space=pl.ANY)
    attended = pl.pallas_call(
        kernel,
        out_shape=jax.ShapeDtypeStruct((8, HEADS * HD), BF16),
        in_specs=[smem, smem, vmem, vmem] + [hbm] * 6,
        out_specs=vmem,
        scratch_shapes=[
            pltpu.VMEM((CHIPS * KDEV, 2 * TOK), BF16),
            pltpu.VMEM((CHIPS, KDEV, WA), BF16),
            pltpu.VMEM((CHIPS, KDEV, WB), BF16),
            pltpu.VMEM((2, TOK, COLS), F32),
            pltpu.VMEM((TOK, COLS), F32),
            pltpu.VMEM((NZ, PARTS, ROWS, COLS), BF16),
            pltpu.VMEM((KVH, SLOTS, PAGE, HD), BF16),
            pltpu.VMEM((KVH, SLOTS, PAGE, HD), BF16),
            pltpu.VMEM((KVH, 2, 2, TAIL, HD), BF16),
            pltpu.VMEM((KVH, 2, 2, TAIL, HD), BF16),
            pltpu.VMEM((NZ, 8, HD), F32),
            pltpu.VMEM((NZ, 8, HD), F32),
            pltpu.VMEM((8, KEYS), F32),
            pltpu.VMEM((8, KEYS), F32),
            pltpu.VMEM((KVH, GROUP * TOK, HD), BF16),
            pltpu.VMEM((HEADS, NZ, 8, HD), F32),
            pltpu.VMEM((2 * KVH, NZ, 8, HD), F32),
            pltpu.VMEM((NCHUNK, GROUP * TOK, CHUNK), F32),
            pltpu.VMEM((NZ, 8, HEADS * HD), BF16),
            pltpu.VMEM((NZ, 8, HD), F32),
            pltpu.VMEM((NZ, 8, HEADS * HD), BF16),
            pltpu.VMEM((NZ, 8, HD), F32),
            pltpu.SemaphoreType.DMA((N_REMOTE,)),
            pltpu.SemaphoreType.DMA((N_REMOTE,)),
            pltpu.SemaphoreType.DMA((3 + 4 * KVH,)),
        ],
        compiler_params=pltpu.CompilerParams(
            collective_id=0, has_side_effects=True, vmem_limit_bytes=56 << 20
        ),
        name="decode",
    )(
        prompt_lengths,
        tail_lengths,
        page_table,
        freq,
        hidden.T,
        w_qkv,
        page_keys,
        page_values,
        tail_keys,
        tail_values,
    )
    return attended.reshape(2, 2, 2, HEADS * HD)


def solution(mesh):
    in_specs = (
        P(None, "row"),
        P("row", "col"),
        P("row", None),
        P("row"),
        P("row", "col", None, None),
        P("row", "col", None, None),
        P("row", None),
        P("row", "col", None, None),
        P("row", "col", None, None),
    )
    out_specs = P("row", "col", None, None)
    return jax.shard_map(
        local_step, mesh=mesh, in_specs=in_specs, out_specs=out_specs, check_vma=False
    )
```

```python
import functools
import math

import jax
import jax.numpy as jnp
import numpy as np
from jax import lax
from jax.experimental import pallas as pl
from jax.experimental.pallas import tpu as pltpu
from jax.sharding import PartitionSpec as P

HEADS = 20
KVH = 4
GROUP = HEADS // KVH
HD = 128
NX = 4
NY = 4
NZ = 8
COLS = 448
WA = 256
WB = COLS - WA
KDEV = 80
CHIPS = NX * NY
TOK = 64
SLOTS = 16
PAGE = 128
KEYS = SLOTS * PAGE
TAIL = 512
CHUNK = 512
NCHUNK = KEYS // CHUNK
SCALE = 1.0 / math.sqrt(HD)
ROPE_BASE = 500000.0
LOW = -1e30
MESH = pl.DeviceIdType.MESH
F32 = jnp.float32
BF16 = jnp.bfloat16

W_COPIES = 8 + 2 + 3 * 4 + 4 * 2
H_COPIES = CHIPS - 1
PARTS = 2
ROWS = TOK // PARTS
Z_COPIES = 7 * PARTS
KCOLS = GROUP * HD
M_COPIES = (KVH // 2 + 1) * (NZ - 1)
N_REMOTE = W_COPIES + H_COPIES + 2 + Z_COPIES + M_COPIES


def nt(a, b):
    return lax.dot_general(a, b, (((1,), (1,)), ((), ())), preferred_element_type=F32)


def iota(shape, axis):
    return lax.broadcasted_iota(jnp.int32, shape, axis)


def kernel(
    lengths,
    tails,
    table,
    freq,
    hidden_t,
    weights,
    page_keys,
    page_values,
    tail_keys,
    tail_values,
    out,
    hbuf,
    wa,
    wb,
    xsend,
    xrecv,
    zall,
    kbuf,
    vbuf,
    tkbuf,
    tvbuf,
    cosb,
    sinb,
    bias,
    tbias,
    qrot,
    qown,
    kvown,
    sbuf,
    pack,
    mlpack,
    racc,
    rml,
    send,
    recv,
    local,
):
    row = lax.axis_index("row")
    z = lax.axis_index("col")
    core = lax.rem(row, 2)
    chip = row // 2
    x = lax.rem(chip, NX)
    y = chip // NX
    first = core == 0

    def plane(a, b):
        dx = jnp.where(first, a, b)
        dy = jnp.where(first, b, a)
        there = lax.rem(y + dy, NY) * NX + lax.rem(x + dx, NX)
        return (there * 2 + core, z)

    def along(d):
        return (row, lax.rem(z + d, NZ))

    sibling = (chip * 2 + 1 - core, z)

    locals_ = []

    def fetch(source, target):
        copy = pltpu.make_async_copy(source, target, local.at[len(locals_)])
        copy.start()
        locals_.append(copy)
        return copy

    own_h = fetch(
        hidden_t.at[:, pl.ds(pl.multiple_of(chip * 128, 128), 128)], hbuf.at[pl.ds(0, KDEV)]
    )
    own_wa = fetch(weights.at[:, pl.ds(0, WA)], wa.at[0])
    own_wb = fetch(weights.at[:, pl.ds(WA, WB)], wb.at[0])

    barrier = pltpu.get_barrier_semaphore()
    for a in range(4):
        for b in range(4):
            if (a, b) != (0, 0):
                pl.semaphore_signal(barrier, inc=1, device_id=plane(a, b), device_id_type=MESH)
    pl.semaphore_signal(barrier, inc=1, device_id=sibling, device_id_type=MESH)
    for d in range(1, NZ):
        pl.semaphore_signal(barrier, inc=1, device_id=along(d), device_id_type=MESH)

    page_copies = []
    for k in range(KVH):
        lanes = pl.ds(k * HD, HD)
        page_copies.append(fetch(page_keys.at[0, :, :, lanes], kbuf.at[k]))
        page_copies.append(fetch(page_values.at[0, :, :, lanes], vbuf.at[k]))
    tail_copies = []
    for k in range(KVH):
        lanes = pl.ds(k * HD, HD)
        tail_copies.append(fetch(tail_keys.at[:, :, :, lanes], tkbuf.at[k]))
        tail_copies.append(fetch(tail_values.at[:, :, :, lanes], tvbuf.at[k]))

    pl.semaphore_wait(barrier, CHIPS + NZ - 1)

    remotes = []

    def push(source, target, device):
        at = len(remotes)
        copy = pltpu.make_async_remote_copy(
            src_ref=source,
            dst_ref=target,
            send_sem=send.at[at],
            recv_sem=recv.at[at],
            device_id=device,
            device_id_type=MESH,
        )
        copy.start()
        remotes.append(copy)
        return copy

    def at(a, b):
        return (a % 4) * 4 + (b % 4)

    def w_push(a, b, half, axis, step):
        da, db = (step, 0) if axis == 0 else (0, step)
        buffer = wa if half == 0 else wb
        there = at(a - da, b - db)
        source = buffer.at[at(a, b)]
        if (a, b) == (0, 0):
            source = weights.at[:, pl.ds(0, WA)] if half == 0 else weights.at[:, pl.ds(WA, WB)]
        return push(source, buffer.at[there], plane(da % 4, db % 4))

    got = {}
    for axis in (0, 1):
        for step in (1, -1):
            for half in (0, 1):
                got["own", axis, step, half] = w_push(0, 0, half, axis, step)
    h_copies = []
    for a, b in sorted(
        [(a, b) for a in range(4) for b in range(4) if (a, b) != (0, 0)],
        key=lambda ab: -(min(ab[0], 4 - ab[0]) + min(ab[1], 4 - ab[1])),
    ):
        device = plane(a, b)
        there = device[0] // 2
        h_copies.append(
            push(
                hidden_t.at[:, pl.ds(pl.multiple_of(there * 128, 128), 128)],
                hbuf.at[pl.ds(at(-a, -b) * KDEV, KDEV)],
                device,
            )
        )

    lane = iota((TOK, HD), 1)
    token = iota((TOK, HD), 0)
    position = jnp.zeros((TOK, HD), jnp.int32)
    for c in range(NZ):
        for p in range(2):
            for s in range(2):
                number = c * 4 + p * 2 + s
                value = lengths[p] + tails[p, 2 * c + s]
                position = jnp.where(token // 2 == number, value, position)
    position = position + lax.rem(token, 2)
    angles = position.astype(F32) * freq[...]
    cosb[...] = jnp.cos(angles).reshape(NZ, 8, HD)
    sines = jnp.sin(angles)
    sinb[...] = jnp.where(lane < HD // 2, -sines, sines).reshape(NZ, 8, HD)

    sub = iota((8, PAGE), 0)
    wide = iota((8, PAGE), 1)
    slot_ids = z * SLOTS + iota((SLOTS, 64), 0)
    starts = iota((SLOTS, 64), 1) * PAGE
    seen = []
    for p in range(2):
        hit = table[p : p + 1, :] == slot_ids
        count = jnp.clip(lengths[p] - starts, 0, PAGE)
        seen.append(jnp.sum(jnp.where(hit, count, 0).astype(F32), axis=1, keepdims=True))
    for j in range(SLOTS):
        limit = jnp.where(sub < 4, seen[0][j : j + 1, :], seen[1][j : j + 1, :])
        bias[:, j * PAGE : (j + 1) * PAGE] = jnp.where(wide.astype(F32) < limit, 0.0, LOW)
    tsub = iota((8, TAIL), 0)
    twide = iota((8, TAIL), 1)
    for p in range(2):
        for s in range(2):
            number = p * 2 + s
            count = tails[p, 2 * z + s]
            shown = (tsub // 2 == number) & (twide < count)
            tbias[:, number * TAIL : (number + 1) * TAIL] = jnp.where(shown, 0.0, LOW)

    def arrived(copy):
        copy.wait_recv()

    for step in (1, -1):
        from_a = -step
        for half in (0, 1):
            arrived(got["own", 0, step, half])
        relay_half = 0 if step == 1 else 1
        got["far", relay_half] = w_push(from_a, 0, relay_half, 0, step)
        for half in (0, 1):
            for up in (1, -1):
                got["col", from_a % 4, up, half] = w_push(from_a, 0, half, 1, up)
    for up in (1, -1):
        for half in (0, 1):
            arrived(got["own", 1, up, half])
        relay_half = 0 if up == 1 else 1
        got["relay", 0, relay_half] = w_push(0, -up, relay_half, 1, up)
    for half in (0, 1):
        arrived(got["far", half])
        for up in (1, -1):
            got["col", 2, up, half] = w_push(2, 0, half, 1, up)
    for a in (3, 1, 2):
        for up in (1, -1):
            for half in (0, 1):
                arrived(got["col", a, up, half])
            relay_half = 0 if up == 1 else 1
            got["relay", a, relay_half] = w_push(a, -up, relay_half, 1, up)
    for copy in h_copies:
        arrived(copy)
    own_h.wait()
    own_wa.wait()
    own_wb.wait()
    for a in (0, 3, 1, 2):
        for half in (0, 1):
            arrived(got["relay", a, half])

    new = iota((2 * TOK, 2 * TOK), 0)
    old = iota((2 * TOK, 2 * TOK), 1)
    wanted = (
        (new // 64) * 64
        + lax.rem(new // 4, 2) * 32
        + (lax.rem(new, 64) // 8) * 4
        + lax.rem(new, 4)
    )
    order = jnp.where(wanted == old, 1.0, 0.0).astype(BF16)
    rows = nt(order, hbuf[...]).astype(BF16)
    swaps = []
    for half, buffer, width in ((0, wa, WA), (1, wb, WB)):
        part = jnp.dot(
            rows, buffer[...].reshape(CHIPS * KDEV, width), preferred_element_type=F32
        )
        xsend[:, :, half * WA : half * WA + width] = part.reshape(2, TOK, width)
        columns = pl.ds(half * WA, width)
        swaps.append(push(xsend.at[1 - core, :, columns], xrecv.at[:, columns], sibling))
    for copy in swaps:
        arrived(copy)
    projected = (xsend[core] + xrecv[...]).astype(BF16)
    zall[z] = projected.reshape(PARTS, ROWS, COLS)

    ring = {}

    def z_push(distance, up, part):
        block = lax.rem(z + NZ - up * distance, NZ)
        ring[distance + 1, up, part] = push(
            zall.at[block, part], zall.at[block, part], along(up % NZ)
        )

    def piece_of(part, up):
        return part if up == 1 else (part + PARTS // 2) % PARTS

    for part in range(PARTS):
        for up in (1, -1):
            z_push(0, up, piece_of(part, up))
    for distance in (1, 2, 3):
        for part in range(PARTS):
            for up in (1, -1):
                piece = piece_of(part, up)
                arrived(ring[distance, up, piece])
                if distance < 3 or part < PARTS // 2:
                    z_push(distance, up, piece)
    for part in range(PARTS // 2):
        for up in (1, -1):
            arrived(ring[4, up, piece_of(part, up)])

    def head_columns(h):
        begin = h * HD
        block, offset = begin // COLS, begin % COLS
        if offset + HD <= COLS:
            return zall[block, :, :, offset : offset + HD].reshape(TOK, HD)
        cut = COLS - offset
        return jnp.concatenate(
            [
                zall[block, :, :, offset:COLS].reshape(TOK, cut),
                zall[block + 1, :, :, 0 : HD - cut].reshape(TOK, HD - cut),
            ],
            axis=1,
        )

    cosine = cosb[...].reshape(TOK, HD)
    signed = sinb[...].reshape(TOK, HD)

    def turn(values, cosine, signed):
        return values * cosine + pltpu.roll(values, HD // 2, 1) * signed

    for h in range(HEADS):
        k, g = h // GROUP, h % GROUP
        turned = turn(head_columns(h).astype(F32), cosine, signed).astype(BF16)
        qrot[k, g * TOK : (g + 1) * TOK, :] = turned
        qown[h] = turned.astype(F32).reshape(NZ, 8, HD)
    for i in range(2 * KVH):
        kvown[i] = head_columns(HEADS + i).astype(F32).reshape(NZ, 8, HD)

    for copy in page_copies:
        copy.wait()

    states = []
    lanes = iota((TOK, HD), 1)
    mlpack[...] = jnp.full((NZ, 8, HD), LOW, F32)

    def attend(k):
        both = mlpack[...].reshape(TOK, HD)
        query = qrot[k]
        best = jnp.full((GROUP * TOK, PAGE), LOW, F32)
        for i in range(NCHUNK):
            keys = kbuf[k, i * 4 : (i + 1) * 4].reshape(CHUNK, HD)
            scores = nt(query, keys) * SCALE
            scores = (
                scores.reshape(GROUP * NZ, 8, CHUNK)
                + bias[:, i * CHUNK : (i + 1) * CHUNK][None]
            ).reshape(GROUP * TOK, CHUNK)
            sbuf[i] = scores
            for n in range(CHUNK // PAGE):
                best = jnp.maximum(best, scores[:, n * PAGE : (n + 1) * PAGE])
        top = jnp.max(best, axis=1, keepdims=True)
        total = jnp.zeros((GROUP * TOK, PAGE), F32)
        acc = jnp.zeros((GROUP * TOK, HD), F32)
        for i in range(NCHUNK):
            e = jnp.exp(sbuf[i] - top)
            for n in range(CHUNK // PAGE):
                total = total + e[:, n * PAGE : (n + 1) * PAGE]
            acc = acc + jnp.dot(
                e.astype(BF16),
                vbuf[k, i * 4 : (i + 1) * 4].reshape(CHUNK, HD),
                preferred_element_type=F32,
            )
        total = jnp.sum(total, axis=1, keepdims=True)
        for g in range(GROUP):
            h = k * GROUP + g
            part = slice(g * TOK, (g + 1) * TOK)
            pack[:, :, h * HD : (h + 1) * HD] = acc[part].reshape(NZ, 8, HD).astype(BF16)
            both = jnp.where(lanes == h, top[part], both)
            both = jnp.where(lanes == h + HD // 2, total[part], both)
        mlpack[...] = both.reshape(NZ, 8, HD)

    for k in range(KVH):
        pl.when(z >= 0)(functools.partial(attend, k))
        if k % 2 == 0:
            continue
        columns = pl.ds((k - 1) * KCOLS, 2 * KCOLS)
        for d in (4, 3, 5, 2, 6, 1, 7):
            there = lax.rem(z + d, NZ)
            source = pack.at[there, :, columns]
            states.append(push(source, racc.at[NZ - d, :, columns], along(d)))
    for d in (4, 3, 5, 2, 6, 1, 7):
        there = lax.rem(z + d, NZ)
        states.append(push(mlpack.at[there], rml.at[NZ - d], along(d)))
    for copy in tail_copies:
        copy.wait()
    fresh_row = iota((8, 16), 0)
    fresh_col = iota((8, 16), 1)
    fresh_shown = (
        (fresh_col < 8)
        & (fresh_row // 2 == fresh_col // 2)
        & (lax.rem(fresh_col, 2) <= lax.rem(fresh_row, 2))
    )
    fresh_bias = jnp.where(fresh_shown, 0.0, LOW)
    nothing = jnp.zeros((8, HD), F32)
    my_cos = cosb[z]
    my_sin = sinb[z]
    small = iota((8, HD), 1)
    own_tops = jnp.full((8, HD), LOW, F32)
    own_sums = jnp.zeros((8, HD), F32)
    own_acc = []
    for k in range(KVH):
        query = jnp.concatenate([qown[k * GROUP + g, z] for g in range(GROUP)], axis=0)
        query = query.astype(BF16)
        new_key = turn(kvown[k, z], my_cos, my_sin)
        new_key = jnp.concatenate([new_key, nothing], axis=0).astype(BF16)
        new_value = jnp.concatenate([kvown[KVH + k, z], nothing], axis=0).astype(BF16)
        scores = nt(query, tkbuf[k].reshape(KEYS, HD)) * SCALE
        scores = scores.reshape(GROUP, 8, KEYS) + tbias[...][None]
        scores = scores.reshape(GROUP * 8, KEYS)
        fresh = nt(query, new_key) * SCALE
        fresh = (fresh.reshape(GROUP, 8, 16) + fresh_bias[None]).reshape(GROUP * 8, 16)
        top = jnp.maximum(
            jnp.max(scores, axis=1, keepdims=True), jnp.max(fresh, axis=1, keepdims=True)
        )
        e = jnp.exp(scores - top)
        f = jnp.exp(fresh - top)
        total = jnp.sum(e, axis=1, keepdims=True) + jnp.sum(f, axis=1, keepdims=True)
        acc = jnp.dot(
            e.astype(BF16), tvbuf[k].reshape(KEYS, HD), preferred_element_type=F32
        ) + jnp.dot(f.astype(BF16), new_value, preferred_element_type=F32)
        for g in range(GROUP):
            h = k * GROUP + g
            part = slice(g * 8, (g + 1) * 8)
            own_acc.append(acc[part])
            own_tops = jnp.where(small == h, top[part], own_tops)
            own_sums = jnp.where(small == h, total[part], own_sums)

    for copy in states:
        arrived(copy)
    racc[0] = pack[z]
    rml[0] = mlpack[z]
    best = own_tops
    for i in range(NZ):
        best = jnp.maximum(best, rml[i])
    factors = [jnp.exp(own_tops - best)]
    total = factors[0] * own_sums
    for i in range(NZ):
        factor = jnp.exp(rml[i] - best)
        factors.append(factor)
        total = total + factor * pltpu.roll(rml[i], HD // 2, 1)
    for h in range(HEADS):
        column = slice(h * HD, (h + 1) * HD)
        acc = factors[0][:, h : h + 1] * own_acc[h]
        for i in range(NZ):
            acc = acc + factors[i + 1][:, h : h + 1] * racc[i, :, column].astype(F32)
        out[:, column] = (acc / total[:, h : h + 1]).astype(BF16)

    for copy in remotes:
        copy.wait_send()


def local_step(
    hidden,
    w_qkv,
    page_table,
    prompt_lengths,
    page_keys,
    page_values,
    tail_lengths,
    tail_keys,
    tail_values,
):
    half = np.arange(HD // 2, dtype=np.float64)
    one = np.exp(half * (-2.0 * math.log(ROPE_BASE) / HD)).astype(np.float32)
    freq = jnp.asarray(np.concatenate([one, one])[None])
    smem = pl.BlockSpec(memory_space=pltpu.SMEM)
    vmem = pl.BlockSpec(memory_space=pltpu.VMEM)
    hbm = pl.BlockSpec(memory_space=pl.ANY)
    attended = pl.pallas_call(
        kernel,
        out_shape=jax.ShapeDtypeStruct((8, HEADS * HD), BF16),
        in_specs=[smem, smem, vmem, vmem] + [hbm] * 6,
        out_specs=vmem,
        scratch_shapes=[
            pltpu.VMEM((CHIPS * KDEV, 2 * TOK), BF16),
            pltpu.VMEM((CHIPS, KDEV, WA), BF16),
            pltpu.VMEM((CHIPS, KDEV, WB), BF16),
            pltpu.VMEM((2, TOK, COLS), F32),
            pltpu.VMEM((TOK, COLS), F32),
            pltpu.VMEM((NZ, PARTS, ROWS, COLS), BF16),
            pltpu.VMEM((KVH, SLOTS, PAGE, HD), BF16),
            pltpu.VMEM((KVH, SLOTS, PAGE, HD), BF16),
            pltpu.VMEM((KVH, 2, 2, TAIL, HD), BF16),
            pltpu.VMEM((KVH, 2, 2, TAIL, HD), BF16),
            pltpu.VMEM((NZ, 8, HD), F32),
            pltpu.VMEM((NZ, 8, HD), F32),
            pltpu.VMEM((8, KEYS), F32),
            pltpu.VMEM((8, KEYS), F32),
            pltpu.VMEM((KVH, GROUP * TOK, HD), BF16),
            pltpu.VMEM((HEADS, NZ, 8, HD), F32),
            pltpu.VMEM((2 * KVH, NZ, 8, HD), F32),
            pltpu.VMEM((NCHUNK, GROUP * TOK, CHUNK), F32),
            pltpu.VMEM((NZ, 8, HEADS * HD), BF16),
            pltpu.VMEM((NZ, 8, HD), F32),
            pltpu.VMEM((NZ, 8, HEADS * HD), BF16),
            pltpu.VMEM((NZ, 8, HD), F32),
            pltpu.SemaphoreType.DMA((N_REMOTE,)),
            pltpu.SemaphoreType.DMA((N_REMOTE,)),
            pltpu.SemaphoreType.DMA((3 + 4 * KVH,)),
        ],
        compiler_params=pltpu.CompilerParams(
            collective_id=0, has_side_effects=True, vmem_limit_bytes=56 << 20
        ),
        name="decode",
    )(
        prompt_lengths,
        tail_lengths,
        page_table,
        freq,
        hidden.T,
        w_qkv,
        page_keys,
        page_values,
        tail_keys,
        tail_values,
    )
    return attended.reshape(2, 2, 2, HEADS * HD)


def solution(mesh):
    in_specs = (
        P(None, "row"),
        P("row", "col"),
        P("row", None),
        P("row"),
        P("row", "col", None, None),
        P("row", "col", None, None),
        P("row", None),
        P("row", "col", None, None),
        P("row", "col", None, None),
    )
    out_specs = P("row", "col", None, None)
    return jax.shard_map(
        local_step, mesh=mesh, in_specs=in_specs, out_specs=out_specs, check_vma=False
    )
```
